512 devices in a mesh: dp: 4 (over x), cand: 32 (over z, core), tensor: 4 (over y).
Axes of the slice: x: 4, y: 4, z: 16, core: 2. Of those that a mesh axis runs over, the one named last changes fastest.
Arguments:
- context: bfloat16 [8, 4096, 3584], P('dp', 'cand', 'tensor'), may hold values from -12 to 12
- residual: bfloat16 [8, 4096, 3584], P('dp', ('cand', 'tensor')), may hold values from -36 to 36
- out_weight: bfloat16 [3584, 3584], P('cand', 'tensor'), may hold values from -0.09375 to 0.09375
- adapter_down: bfloat16 [3584, 16], P('tensor'), may hold values from -0.09375 to 0.09375
- adapter_up_weight: bfloat16 [16, 3584], replicated, may hold values from -1.5 to 1.5
- norm_gain: float32 [3584], replicated, may hold values from 0.5 to 1.5
- score_weight: float32 [3584], replicated, may hold values from -0.09375 to 0.09375
- teacher: bfloat16 [8, 4096, 4096], P('dp', 'cand', 'tensor'), may hold values from 0.019897461 to 0.9765625
- pair_mask: int32 [8, 4096, 4096], P('dp', 'cand', 'tensor'), may hold values from 0 to 1, as said below
- loss_scale: float32 [8], P('dp'), may hold values from 65536 to 262144
Outputs:
- context_grad: bfloat16 [8, 4096, 3584], P('dp', 'cand', 'tensor')
- residual_gradient: bfloat16 [8, 4096, 3584], P('dp', ('cand', 'tensor'))
- down_grad: float32 [3584, 16], P('tensor')
- up_weight_gradient: float32 [16, 3584], P(None, 'tensor')
- pair_loss: float32 [8], P('dp')
The draws below stay inside these ranges and needn't reach their ends.
Inputs may be any that keep to these rules, and one draw needn't show every extreme that they name: pair_mask holds 0 or 1; with P = 32, every pair (i, j) whose group j // P lies 4096 / (2P) groups after i // P, counted round over the 4096 / P groups, is valid.
All inputs are finite; a program needn't handle non-finite values.
Results may differ from the reference program's by a relative error of at most 0.02.
Values may be sent and summed in bfloat16 or wider, within the bound.
No kernel may reach another device: no remote copies, remote signals or barrier semaphores. Data moves between devices by JAX's collectives and lax.ppermute only.
A program may use at most 64 MiB of HBM per device.

```python
import math
import jax
import jax.numpy as jnp
from jax import lax

MODEL_WIDTH = 3584
RANK = 16
C_DEV = 128
H = 3584
HB = 896
NC = 4096
QUERIES = 8


def shared_rows(key):
    levels = jax.random.uniform(jax.random.fold_in(key, 7), (QUERIES, NC, 1), jnp.float32, math.log(0.3), math.log(3.0))
    return jnp.exp(levels)


def noise(key, shape):
    return jnp.clip(jax.random.normal(key, shape, jnp.float32), -4.0, 4.0)


def draw_context(key, part):
    values = noise(jax.random.fold_in(key, 13), (QUERIES, NC, H)) * shared_rows(key)
    return values.astype(jnp.bfloat16)


def draw_residual(key, part):
    columns = jnp.exp(jax.random.uniform(jax.random.fold_in(key, 41), (MODEL_WIDTH,), jnp.float32, math.log(0.3), math.log(3.0)))
    values = noise(jax.random.fold_in(key, 31), (QUERIES, NC, MODEL_WIDTH)) * shared_rows(key) * columns
    return values.astype(jnp.bfloat16)


def draw_pair_mask(key, part):
    row_ids = lax.broadcasted_iota(jnp.int32, (QUERIES, NC, NC), 1)
    col_ids = lax.broadcasted_iota(jnp.int32, (QUERIES, NC, NC), 2)
    levels = jax.random.randint(jax.random.fold_in(key, 51), (QUERIES, NC, NC), 0, 32 * NC)
    live = (levels < NC + 2 * row_ids).astype(jnp.int32)
    group_size = C_DEV * HB // H
    group_count = NC // group_size
    offset = (col_ids // group_size - row_ids // group_size + group_count) % group_count
    band = (offset == group_count // 2).astype(jnp.int32)
    return jnp.maximum(live, band)


def steps_of(own_key, shape, shards, smallest, largest):
    def one(axis_at, blocks):
        heights = jax.random.uniform(jax.random.fold_in(jax.random.fold_in(own_key, 6), axis_at), (blocks,), jnp.float32, smallest / len(shards), largest / len(shards))
        return jnp.repeat(jnp.exp(heights), shape[axis_at] // blocks).reshape((-1,) + (1,) * (len(shape) - axis_at - 1))

    gain = one(*shards[0])
    for cut in shards[1:]:
        gain = gain * one(*cut)
    return gain


def scatter_about(stream_key, shape, spread, reach, split=(), dtype=jnp.bfloat16):
    loudness = steps_of(stream_key, shape, split, -0.22, 0.18) if split else 1.0
    result = jax.random.normal(stream_key, shape, jnp.float32) * spread * loudness
    return jnp.minimum(jnp.maximum(result, -reach), reach).astype(dtype)


def setup_inputs(seed: int = 0) -> dict:
    key_list = jax.random.split(jax.random.key(seed), 11)
    context = draw_context(jax.random.fold_in(key_list[10], 71), 0)
    residual = draw_residual(jax.random.fold_in(key_list[10], 71), 0)
    out_weight = scatter_about(key_list[2], (MODEL_WIDTH, H), H ** -0.5, 0.09375, ((0, 32), (1, 4)))
    adapter_down = scatter_about(key_list[3], (H, RANK), H ** -0.5, 0.09375, ((0, 4),))
    adapter_up_weight = scatter_about(key_list[4], (RANK, MODEL_WIDTH), RANK ** -0.5, 1.5)
    norm_gain = jnp.clip(1.0 + 0.1 * jax.random.normal(key_list[5], (MODEL_WIDTH,), jnp.float32), 0.5, 1.5)
    score_weight = scatter_about(key_list[6], (MODEL_WIDTH,), MODEL_WIDTH ** -0.5, 0.09375, (), jnp.float32)
    teacher = jnp.clip(0.019897461 + 0.95666504 * jax.random.uniform(key_list[7], (QUERIES, NC, NC), jnp.float32) ** steps_of(key_list[7], (QUERIES, NC, NC), ((0, 4), (1, 32), (2, 4)), -0.2, 0.2), 0.019897461, 0.9765625).astype(jnp.bfloat16)
    pair_mask = draw_pair_mask(jax.random.fold_in(key_list[10], 71), 0)
    loss_scale = jnp.clip(jnp.exp(math.log(262144.0) - 1.3862944 * jax.random.uniform(key_list[9], (QUERIES,), jnp.float32) ** steps_of(key_list[9], (QUERIES,), ((0, 4),), -0.2, 0.2)), 65536.0, 262144.0)
    return {"context": context, "residual": residual, "out_weight": out_weight, "adapter_down": adapter_down, "adapter_up_weight": adapter_up_weight, "norm_gain": norm_gain, "score_weight": score_weight, "teacher": teacher, "pair_mask": pair_mask, "loss_scale": loss_scale}


ADAPTER_SCALE = 0.5
epsilon = 1e-06

def pair_query(inputs):
    scores, target, valid = inputs
    margin = scores[:, None] - scores[None, :]
    valid_pairs = valid.astype(jnp.float32)
    target_f = target.astype(jnp.float32)
    total = jnp.sum(valid_pairs * (jax.nn.softplus(margin) - target_f * margin))
    count = jnp.sum(valid_pairs)
    slope = valid_pairs * (jax.nn.sigmoid(margin) - target_f)
    return (total, count, lax.optimization_barrier(jnp.sum(slope, axis=1)) - lax.optimization_barrier(jnp.sum(slope, axis=0)))

def reference(context, residual, out_weight, adapter_down, adapter_up_weight, norm_gain, score_weight, teacher, pair_mask, loss_scale):
    total_row_count = QUERIES * NC
    flat = context.reshape(total_row_count, H)
    head_total_sum = jnp.zeros((total_row_count, MODEL_WIDTH), jnp.float32)
    low_sum = jnp.zeros((total_row_count, RANK), jnp.float32)
    for block in range(H // HB):
        lower = block * HB
        slab = flat[:, lower:lower + HB]
        head_term = jnp.dot(slab, out_weight[:, lower:lower + HB].T, preferred_element_type=jnp.float32)
        head_total_sum = head_total_sum + lax.optimization_barrier(head_term.astype(jnp.bfloat16)).astype(jnp.float32)
        low_term = jnp.dot(slab, adapter_down[lower:lower + HB, :], preferred_element_type=jnp.float32)
        low_sum = low_sum + lax.optimization_barrier(low_term.astype(jnp.bfloat16)).astype(jnp.float32)
    adapter_input_rows = low_sum.astype(jnp.bfloat16)
    lifted_rows = jnp.dot(adapter_input_rows, adapter_up_weight, preferred_element_type=jnp.float32)
    hidden_state = (residual.reshape(total_row_count, MODEL_WIDTH).astype(jnp.float32) + head_total_sum + ADAPTER_SCALE * lifted_rows).astype(jnp.bfloat16)
    hidden_wide = hidden_state.astype(jnp.float32)
    inv_rms = lax.rsqrt(lax.optimization_barrier(jnp.mean(hidden_wide * hidden_wide, axis=1, keepdims=True)) + epsilon)
    scores = lax.optimization_barrier(jnp.sum(hidden_wide * inv_rms * norm_gain * score_weight, axis=1)).reshape(QUERIES, NC)
    totals, counts, raw_grad = lax.map(pair_query, (scores, teacher, pair_mask))
    pair_loss = totals / counts
    score_grad = raw_grad * (loss_scale / counts)[:, None]
    back_step = score_grad.reshape(total_row_count, 1) * norm_gain * score_weight
    grad_hidden = inv_rms * back_step - hidden_wide * inv_rms ** 3 * lax.optimization_barrier(jnp.mean(hidden_wide * back_step, axis=1, keepdims=True))
    residual_gradient = grad_hidden.astype(jnp.bfloat16)
    adapter_input_gradient = (ADAPTER_SCALE * jnp.dot(residual_gradient, adapter_up_weight.T, preferred_element_type=jnp.float32)).astype(jnp.bfloat16)
    context_grad = (jnp.dot(residual_gradient, out_weight, preferred_element_type=jnp.float32) + jnp.dot(adapter_input_gradient, adapter_down.T, preferred_element_type=jnp.float32)).astype(jnp.bfloat16)
    down_grad = jnp.dot(flat.T, adapter_input_gradient, preferred_element_type=jnp.float32)
    up_weight_gradient = ADAPTER_SCALE * jnp.dot(adapter_input_rows.T, residual_gradient, preferred_element_type=jnp.float32)
    return (context_grad.reshape(QUERIES, NC, H), residual_gradient.reshape(QUERIES, NC, MODEL_WIDTH), down_grad, up_weight_gradient, pair_loss)
```

```python
import jax
import jax.numpy as jnp
from jax import lax
from jax.sharding import PartitionSpec as P

ADAPTER_SCALE = 0.5
epsilon = 1e-06
F32 = jnp.float32
BF16 = jnp.bfloat16


def on_device(
    context,
    residual,
    out_weight,
    adapter_down,
    adapter_up_weight,
    norm_gain,
    score_weight,
    teacher,
    pair_mask,
    loss_scale,
):
    queries, cand_rows, _ = context.shape
    width = residual.shape[2]
    cols = teacher.shape[2]
    tensor_count = lax.axis_size("tensor")
    cand_count = lax.axis_size("cand")
    share = cand_rows // tensor_count
    near = cols // cand_rows
    tensor_index = lax.axis_index("tensor")
    dp_index = lax.axis_index("dp")

    full_weight = lax.all_gather(out_weight, "cand", axis=0, tiled=True)

    low_terms = jnp.einsum(
        "qch,hr->qcr", context, adapter_down, preferred_element_type=F32
    ).astype(BF16)
    low_all = lax.all_gather(low_terms, "tensor", axis=0)
    adapter_in = jnp.sum(low_all.astype(F32), axis=0).astype(BF16)
    adapter_own = lax.dynamic_slice_in_dim(adapter_in, tensor_index * share, share, 1)
    lifted = jnp.einsum("qcr,rd->qcd", adapter_own, adapter_up_weight, preferred_element_type=F32)
    base = residual.astype(F32) + ADAPTER_SCALE * lifted

    valid = pair_mask.astype(F32)
    target = teacher.astype(F32)
    mask_count = jnp.sum(valid, axis=(1, 2))
    row_known = jnp.sum(valid * target, axis=2)
    col_known = jnp.sum(valid * (1.0 - target), axis=1)
    groups = [[a * near + b for b in range(near)] for a in range(cand_count // near)]
    swap = [
        ((a * near + b) * tensor_count + t, (t * near + b) * tensor_count + a)
        for a in range(cand_count // near)
        for b in range(near)
        for t in range(tensor_count)
    ]
    blocks = jnp.swapaxes(
        pair_mask.astype(BF16).reshape(queries, cand_rows, near, cand_rows), 1, 2
    )
    blocks = jnp.swapaxes(blocks, 2, 3)
    blocks = jnp.swapaxes(blocks, 0, 1)
    blocks = lax.all_to_all(
        blocks, "cand", 0, 0, axis_index_groups=groups, tiled=True
    )
    blocks = lax.ppermute(blocks, ("cand", "tensor"), swap)
    other_valid = jnp.moveaxis(blocks, 0, 2).reshape(queries, cand_rows, cols)
    col_known = jnp.swapaxes(col_known.reshape(queries, near, cand_rows), 0, 1)
    col_known = lax.all_to_all(
        col_known, "cand", 0, 0, axis_index_groups=groups, tiled=True
    )
    col_known = lax.ppermute(jnp.sum(col_known, axis=0), ("cand", "tensor"), swap)
    both = valid + other_valid.astype(F32)
    known = row_known + col_known

    full_weight, adapter_in, base, both, known, mask_count = lax.optimization_barrier(
        (full_weight, adapter_in, base, both, known, mask_count)
    )

    by_owner = jnp.swapaxes(
        context.reshape(queries, tensor_count, share, context.shape[2]), 0, 1
    )
    head_terms = jnp.einsum(
        "tqch,dh->tqcd", by_owner, full_weight, preferred_element_type=F32
    ).astype(BF16)
    head_terms = lax.all_to_all(head_terms, "tensor", 0, 0, tiled=True)
    hidden = (base + jnp.sum(head_terms.astype(F32), axis=0)).astype(BF16).astype(F32)
    inv_rms = lax.rsqrt(jnp.mean(hidden * hidden, axis=2) + epsilon)
    gain = norm_gain * score_weight
    dot = jnp.sum(hidden * gain, axis=2)
    scores = dot * inv_rms
    slant = inv_rms * inv_rms * dot / width
    unit = inv_rms[:, :, None] * (gain - hidden * slant[:, :, None])

    unit_sent, unit, scores = lax.optimization_barrier((unit.astype(BF16), unit, scores))
    unit_all = lax.all_gather(unit_sent, "tensor", axis=1, tiled=True)
    message = jnp.concatenate([scores, mask_count[:, None]], axis=1)
    message = lax.all_gather(message, "tensor", axis=0)
    own_scores = jnp.swapaxes(message[:, :, :share], 0, 1).reshape(queries, cand_rows)
    message = jnp.concatenate([own_scores, jnp.sum(message[:, :, share], axis=0)[:, None]], axis=1)
    message = lax.all_gather(message, "cand", axis=0)
    count = jnp.sum(message[:, :, cand_rows], axis=0)
    col_scores = lax.dynamic_slice_in_dim(message, tensor_index * near, near, 0)
    col_scores = jnp.swapaxes(col_scores[:, :, :cand_rows], 0, 1).reshape(queries, cols)

    margin = own_scores[:, :, None] - col_scores[:, None, :]
    raw = jnp.sum(both * jax.nn.sigmoid(margin), axis=2) - known
    total = jnp.sum(valid * (jax.nn.softplus(margin) - target * margin), axis=(1, 2))
    sums = lax.psum(jnp.concatenate([raw, total[:, None]], axis=1), "tensor")
    score_grad = sums[:, :cand_rows] * (loss_scale / count)[:, None]

    own_grad = lax.dynamic_slice_in_dim(score_grad, tensor_index * share, share, 1)
    grad_rows = (own_grad[:, :, None] * unit).astype(BF16)

    adapter_unit = ADAPTER_SCALE * jnp.einsum(
        "qcd,rd->qcr", unit_all, adapter_up_weight, preferred_element_type=F32
    )
    context_unit = jnp.einsum(
        "qcd,dh->qch", unit_all, full_weight, preferred_element_type=F32
    ) + jnp.einsum("qcr,hr->qch", adapter_unit.astype(BF16), adapter_down, preferred_element_type=F32)
    context_grad = (score_grad[:, :, None] * context_unit).astype(BF16)
    adapter_back = (score_grad[:, :, None] * adapter_unit).astype(BF16)
    down_local = jnp.einsum("qcr,qch->rh", adapter_back, context, preferred_element_type=F32)
    block = lax.dynamic_slice_in_dim(
        unit_all, tensor_index * context.shape[2], context.shape[2], 2
    )
    block = (score_grad[:, :, None] * block.astype(F32)).astype(BF16)
    up_local = ADAPTER_SCALE * jnp.einsum(
        "qcr,qcd->rd", adapter_in, block, preferred_element_type=F32
    )

    slots = jnp.zeros((128,), F32)
    slots = lax.dynamic_update_slice_in_dim(slots, sums[:, cand_rows], dp_index * queries, 0)
    flat = jnp.concatenate([down_local, up_local], axis=0)
    columns = flat.shape[1]
    flat = jnp.concatenate([flat, jnp.broadcast_to(slots, (flat.shape[0], 128))], axis=1)
    pieces = lax.all_to_all(flat, "cand", 0, 0, tiled=True)
    piece = jnp.sum(pieces.reshape(cand_count, -1, flat.shape[1]), axis=0)
    piece = lax.psum(piece, "dp")
    flat = lax.all_gather(piece[:, :columns], "cand", axis=0, tiled=True)
    rank = adapter_down.shape[1]
    down_grad = flat[:rank].T
    up_weight_gradient = flat[rank:]
    loss_sum = lax.dynamic_slice_in_dim(piece[0, columns:], dp_index * queries, queries, 0)
    pair_loss = loss_sum / count
    return (context_grad, grad_rows, down_grad, up_weight_gradient, pair_loss)


def solution(mesh):
    in_specs = (
        P("dp", "cand", "tensor"),
        P("dp", ("cand", "tensor"), None),
        P("cand", "tensor"),
        P("tensor", None),
        P(),
        P(),
        P(),
        P("dp", "cand", "tensor"),
        P("dp", "cand", "tensor"),
        P("dp"),
    )
    out_specs = (
        P("dp", "cand", "tensor"),
        P("dp", ("cand", "tensor"), None),
        P("tensor", None),
        P(None, "tensor"),
        P("dp"),
    )
    return jax.shard_map(
        on_device, mesh=mesh, in_specs=in_specs, out_specs=out_specs, check_vma=False
    )
```

```python
import jax
import jax.numpy as jnp
from jax import lax
from jax.sharding import PartitionSpec as P

ADAPTER_SCALE = 0.5
epsilon = 1e-06
F32 = jnp.float32
BF16 = jnp.bfloat16


def gather_copies(x, axis):
    copies = jnp.broadcast_to(x[None], (lax.axis_size(axis),) + x.shape)
    return lax.all_to_all(copies, axis, 0, 0, tiled=True)


def on_device(
    context,
    residual,
    out_weight,
    adapter_down,
    adapter_up_weight,
    norm_gain,
    score_weight,
    teacher,
    pair_mask,
    loss_scale,
):
    queries, cand_rows, _ = context.shape
    width = residual.shape[2]
    cols = teacher.shape[2]
    tensor_count = lax.axis_size("tensor")
    cand_count = lax.axis_size("cand")
    share = cand_rows // tensor_count
    near = cols // cand_rows
    tensor_index = lax.axis_index("tensor")
    dp_index = lax.axis_index("dp")

    full_weight = lax.all_gather(out_weight, "cand", axis=0, tiled=True)

    low_terms = jnp.einsum(
        "qch,hr->qcr", context, adapter_down, preferred_element_type=F32
    ).astype(BF16)
    low_all = lax.all_gather(low_terms, "tensor", axis=0)
    adapter_in = jnp.sum(low_all.astype(F32), axis=0).astype(BF16)
    adapter_own = lax.dynamic_slice_in_dim(adapter_in, tensor_index * share, share, 1)
    lifted = jnp.einsum("qcr,rd->qcd", adapter_own, adapter_up_weight, preferred_element_type=F32)
    base = residual.astype(F32) + ADAPTER_SCALE * lifted

    valid = pair_mask.astype(F32)
    target = teacher.astype(F32)
    mask_count = jnp.sum(valid, axis=(1, 2))

    full_weight, adapter_in, base, mask_count = lax.optimization_barrier(
        (full_weight, adapter_in, base, mask_count)
    )

    by_owner = jnp.swapaxes(
        context.reshape(queries, tensor_count, share, context.shape[2]), 0, 1
    )
    head_terms = jnp.einsum(
        "tqch,dh->tqcd", by_owner, full_weight, preferred_element_type=F32
    ).astype(BF16)
    head_terms = lax.all_to_all(head_terms, "tensor", 0, 0, tiled=True)
    hidden = (base + jnp.sum(head_terms.astype(F32), axis=0)).astype(BF16).astype(F32)
    inv_rms = lax.rsqrt(jnp.mean(hidden * hidden, axis=2) + epsilon)
    gain = norm_gain * score_weight
    dot = jnp.sum(hidden * gain, axis=2)
    scores = dot * inv_rms
    slant = inv_rms * inv_rms * dot / width
    unit = inv_rms[:, :, None] * (gain - hidden * slant[:, :, None])

    unit_sent, unit, scores = lax.optimization_barrier((unit.astype(BF16), unit, scores))
    unit_all = lax.all_gather(unit_sent, "tensor", axis=1, tiled=True)
    message = jnp.concatenate([scores, mask_count[:, None]], axis=1)
    message = lax.all_gather(message, "tensor", axis=0)
    own_scores = jnp.swapaxes(message[:, :, :share], 0, 1).reshape(queries, cand_rows)
    message = jnp.concatenate(
        [own_scores, jnp.broadcast_to(jnp.sum(message[:, :, share], axis=0)[:, None], (queries, 128))],
        axis=1,
    )
    message = gather_copies(message, "cand")
    count = jnp.sum(message[:, :, cand_rows], axis=0)
    col_scores = lax.dynamic_slice_in_dim(message, tensor_index * near, near, 0)
    col_scores = jnp.swapaxes(col_scores[:, :, :cand_rows], 0, 1).reshape(queries, cols)

    margin = own_scores[:, :, None] - col_scores[:, None, :]
    slope = valid * (jax.nn.sigmoid(margin) - target)
    total = jnp.sum(valid * (jax.nn.softplus(margin) - target * margin), axis=(1, 2))
    columns = jnp.swapaxes(jnp.sum(slope, axis=1).reshape(queries, near, cand_rows), 0, 1)
    columns = lax.dynamic_update_slice_in_dim(
        jnp.zeros((cand_count, queries, cand_rows), F32), columns, tensor_index * near, 0
    )
    columns = lax.all_to_all(columns, "cand", 0, 0, tiled=True)
    raw = jnp.sum(slope, axis=2) - jnp.sum(columns, axis=0)
    sums = lax.psum(jnp.concatenate([raw, total[:, None]], axis=1), "tensor")
    score_grad = sums[:, :cand_rows] * (loss_scale / count)[:, None]

    own_grad = lax.dynamic_slice_in_dim(score_grad, tensor_index * share, share, 1)
    grad_rows = (own_grad[:, :, None] * unit).astype(BF16)

    adapter_unit = ADAPTER_SCALE * jnp.einsum(
        "qcd,rd->qcr", unit_all, adapter_up_weight, preferred_element_type=F32
    )
    context_unit = jnp.einsum(
        "qcd,dh->qch", unit_all, full_weight, preferred_element_type=F32
    ) + jnp.einsum("qcr,hr->qch", adapter_unit.astype(BF16), adapter_down, preferred_element_type=F32)
    context_grad = (score_grad[:, :, None] * context_unit).astype(BF16)
    adapter_back = (score_grad[:, :, None] * adapter_unit).astype(BF16)
    down_local = jnp.einsum("qcr,qch->rh", adapter_back, context, preferred_element_type=F32)
    block = lax.dynamic_slice_in_dim(
        unit_all, tensor_index * context.shape[2], context.shape[2], 2
    )
    block = (score_grad[:, :, None] * block.astype(F32)).astype(BF16)
    up_local = ADAPTER_SCALE * jnp.einsum(
        "qcr,qcd->rd", adapter_in, block, preferred_element_type=F32
    )

    slots = jnp.zeros((128,), F32)
    slots = lax.dynamic_update_slice_in_dim(slots, sums[:, cand_rows], dp_index * queries, 0)
    flat = jnp.concatenate([down_local, up_local], axis=0)
    wide = flat.shape[1]
    flat = jnp.concatenate([flat, jnp.broadcast_to(slots, (flat.shape[0], 128))], axis=1)
    pieces = lax.all_to_all(flat, "cand", 0, 0, tiled=True)
    piece = jnp.sum(pieces.reshape(cand_count, -1, flat.shape[1]), axis=0)
    piece = lax.psum(piece, "dp")
    flat = gather_copies(piece[:, :wide], "cand").reshape(flat.shape[0], wide)
    rank = adapter_down.shape[1]
    down_grad = flat[:rank].T
    up_weight_gradient = flat[rank:]
    loss_sum = lax.dynamic_slice_in_dim(piece[0, wide:], dp_index * queries, queries, 0)
    pair_loss = loss_sum / count
    return (context_grad, grad_rows, down_grad, up_weight_gradient, pair_loss)


def solution(mesh):
    in_specs = (
        P("dp", "cand", "tensor"),
        P("dp", ("cand", "tensor"), None),
        P("cand", "tensor"),
        P("tensor", None),
        P(),
        P(),
        P(),
        P("dp", "cand", "tensor"),
        P("dp", "cand", "tensor"),
        P("dp"),
    )
    out_specs = (
        P("dp", "cand", "tensor"),
        P("dp", ("cand", "tensor"), None),
        P("tensor", None),
        P(None, "tensor"),
        P("dp"),
    )
    return jax.shard_map(
        on_device, mesh=mesh, in_specs=in_specs, out_specs=out_specs, check_vma=False
    )
```

```python
import jax
import jax.numpy as jnp
from jax import lax
from jax.sharding import PartitionSpec as P

ADAPTER_SCALE = 0.5
epsilon = 1e-06
F32 = jnp.float32
BF16 = jnp.bfloat16


def gather_copies(x, axis):
    copies = jnp.broadcast_to(x[None], (lax.axis_size(axis),) + x.shape)
    return lax.all_to_all(copies, axis, 0, 0, tiled=True)


def on_device(
    context,
    residual,
    out_weight,
    adapter_down,
    adapter_up_weight,
    norm_gain,
    score_weight,
    teacher,
    pair_mask,
    loss_scale,
):
    queries, cand_rows, _ = context.shape
    width = residual.shape[2]
    cols = teacher.shape[2]
    tensor_count = lax.axis_size("tensor")
    cand_count = lax.axis_size("cand")
    share = cand_rows // tensor_count
    near = cols // cand_rows
    tensor_index = lax.axis_index("tensor")
    dp_index = lax.axis_index("dp")
    cand_index = lax.axis_index("cand")
    dp_count = lax.axis_size("dp")

    full_weight = lax.all_gather(out_weight, "cand", axis=0, tiled=True)

    low_terms = jnp.einsum(
        "qch,hr->qcr", context, adapter_down, preferred_element_type=F32
    ).astype(BF16)
    low_all = lax.all_gather(low_terms, "tensor", axis=0)
    adapter_in = jnp.sum(low_all.astype(F32), axis=0).astype(BF16)
    adapter_own = lax.dynamic_slice_in_dim(adapter_in, tensor_index * share, share, 1)
    lifted = jnp.einsum("qcr,rd->qcd", adapter_own, adapter_up_weight, preferred_element_type=F32)
    base = residual.astype(F32) + ADAPTER_SCALE * lifted

    valid = pair_mask.astype(F32)
    target = teacher.astype(F32)
    mask_count = jnp.sum(valid, axis=(1, 2))
    mask_rows = pair_mask.astype(BF16).reshape(queries, tensor_count, share, cols)
    mask_rows = lax.all_to_all(jnp.swapaxes(mask_rows, 0, 1), "tensor", 0, 0, tiled=True)
    mask_rows = mask_rows.reshape(tensor_count, queries, share, near, cand_rows)
    mask_rows = jnp.moveaxis(mask_rows, 3, 1).reshape(cand_count, queries, share, cand_rows)
    known = jnp.swapaxes(jnp.sum(valid * target, axis=1).reshape(queries, near, cand_rows), 0, 1)
    known = lax.dynamic_update_slice_in_dim(
        jnp.zeros((cand_count, queries, cand_rows), F32), known, tensor_index * near, 0
    )
    known = jnp.sum(lax.all_to_all(known, "cand", 0, 0, tiled=True), axis=0)

    full_weight, adapter_in, base, mask_count, mask_rows, known = lax.optimization_barrier(
        (full_weight, adapter_in, base, mask_count, mask_rows, known)
    )

    head_terms = jnp.einsum(
        "qch,dh->qcd", context, full_weight, preferred_element_type=F32
    ).astype(BF16)
    head_terms, mask_rows = lax.optimization_barrier((head_terms, mask_rows))
    head_sum = lax.psum_scatter(head_terms, "tensor", scatter_dimension=1, tiled=True)
    turned = lax.all_to_all(mask_rows, "cand", 0, 0, tiled=True)
    head_sum, turned = lax.optimization_barrier((head_sum, turned))
    hidden = (base + head_sum.astype(F32)).astype(BF16).astype(F32)
    inv_rms = lax.rsqrt(jnp.mean(hidden * hidden, axis=2) + epsilon)
    gain = norm_gain * score_weight
    dot = jnp.sum(hidden * gain, axis=2)
    scores = dot * inv_rms
    slant = inv_rms * inv_rms * dot / width
    unit = inv_rms[:, :, None] * (gain - hidden * slant[:, :, None])

    unit_sent, unit, scores = lax.optimization_barrier((unit.astype(BF16), unit, scores))
    unit_all = lax.all_gather(unit_sent, "tensor", axis=1, tiled=True)
    message = jnp.concatenate(
        [scores, jnp.broadcast_to(mask_count[:, None], (queries, 128 - share))], axis=1
    )
    message = gather_copies(message, ("cand", "tensor"))
    count = jnp.sum(message[:, :, share], axis=0)
    message = message[:, :, :share].reshape(cand_count, tensor_count, queries, share)
    all_scores = jnp.moveaxis(message, 2, 0).reshape(queries, cand_count * cand_rows)
    own_scores = lax.dynamic_slice_in_dim(all_scores, cand_index * cand_rows, cand_rows, 1)
    col_scores = lax.dynamic_slice_in_dim(all_scores, tensor_index * cols, cols, 1)
    turned_scores = lax.dynamic_index_in_dim(message, tensor_index, 1, keepdims=False)

    margin = own_scores[:, :, None] - col_scores[:, None, :]
    slope = valid * (jax.nn.sigmoid(margin) - target)
    total = jnp.sum(valid * (jax.nn.softplus(margin) - target * margin), axis=(1, 2))
    turned_margin = turned_scores[:, :, :, None] - own_scores[None, :, None, :]
    turned_sum = jnp.sum(turned.astype(F32) * jax.nn.sigmoid(turned_margin), axis=(0, 2))
    raw = jnp.sum(slope, axis=2) - (turned_sum - known)
    raw, unit_all = lax.optimization_barrier((raw, unit_all))
    sums = lax.psum(jnp.concatenate([raw, total[:, None]], axis=1), "tensor")
    score_grad = sums[:, :cand_rows] * (loss_scale / count)[:, None]

    own_grad = lax.dynamic_slice_in_dim(score_grad, tensor_index * share, share, 1)
    grad_rows = (own_grad[:, :, None] * unit).astype(BF16)

    adapter_unit = ADAPTER_SCALE * jnp.einsum(
        "qcd,rd->qcr", unit_all, adapter_up_weight, preferred_element_type=F32
    )
    context_unit = jnp.einsum(
        "qcd,dh->qch", unit_all, full_weight, preferred_element_type=F32
    ) + jnp.einsum("qcr,hr->qch", adapter_unit.astype(BF16), adapter_down, preferred_element_type=F32)
    context_grad = (score_grad[:, :, None] * context_unit).astype(BF16)
    adapter_back = (score_grad[:, :, None] * adapter_unit).astype(BF16)
    down_local = jnp.einsum("qcr,qch->rh", adapter_back, context, preferred_element_type=F32)
    block = lax.dynamic_slice_in_dim(
        unit_all, tensor_index * context.shape[2], context.shape[2], 2
    )
    block = (score_grad[:, :, None] * block.astype(F32)).astype(BF16)
    up_local = ADAPTER_SCALE * jnp.einsum(
        "qcr,qcd->rd", adapter_in, block, preferred_element_type=F32
    )

    rank = adapter_down.shape[1]
    flat = jnp.concatenate([down_local, up_local], axis=0)
    slots = jnp.zeros((1, 128), F32)
    slots = lax.dynamic_update_slice_in_dim(slots, sums[None, :, cand_rows], dp_index * queries, 1)
    tiles = flat.shape[1] // 128
    devices = dp_count * cand_count
    rows = (tiles + 1) * 2 * rank
    rows += -rows % devices
    pad = jnp.zeros((rows - 2 * rank * tiles - 1, 128), F32)
    flat = jnp.swapaxes(flat.reshape(2 * rank, tiles, 128), 0, 1).reshape(-1, 128)
    flat = jnp.concatenate([flat, slots, pad])
    pieces = lax.all_to_all(flat.reshape(devices, -1, 128), ("dp", "cand"), 0, 0, tiled=True)
    flat = gather_copies(jnp.sum(pieces, axis=0), ("dp", "cand")).reshape(rows, 128)
    loss_sum = lax.dynamic_slice_in_dim(flat[2 * rank * tiles], dp_index * queries, queries, 0)
    pair_loss = loss_sum / count
    flat = flat[: 2 * rank * tiles].reshape(tiles, 2 * rank, 128)
    flat = jnp.swapaxes(flat, 0, 1).reshape(2 * rank, 128 * tiles)
    down_grad = flat[:rank].T
    up_weight_gradient = flat[rank:]
    return (context_grad, grad_rows, down_grad, up_weight_gradient, pair_loss)


def solution(mesh):
    in_specs = (
        P("dp", "cand", "tensor"),
        P("dp", ("cand", "tensor"), None),
        P("cand", "tensor"),
        P("tensor", None),
        P(),
        P(),
        P(),
        P("dp", "cand", "tensor"),
        P("dp", "cand", "tensor"),
        P("dp"),
    )
    out_specs = (
        P("dp", "cand", "tensor"),
        P("dp", ("cand", "tensor"), None),
        P("tensor", None),
        P(None, "tensor"),
        P("dp"),
    )
    return jax.shard_map(
        on_device, mesh=mesh, in_specs=in_specs, out_specs=out_specs, check_vma=False
    )
```

```python
import jax
import jax.numpy as jnp
from jax import lax
from jax.sharding import PartitionSpec as P

ADAPTER_SCALE = 0.5
epsilon = 1e-06
F32 = jnp.float32
BF16 = jnp.bfloat16


def gather_copies(x, axis):
    copies = jnp.broadcast_to(x[None], (lax.axis_size(axis),) + x.shape)
    return lax.all_to_all(copies, axis, 0, 0, tiled=True)


def on_device(
    context,
    residual,
    out_weight,
    adapter_down,
    adapter_up_weight,
    norm_gain,
    score_weight,
    teacher,
    pair_mask,
    loss_scale,
):
    queries, cand_rows, _ = context.shape
    width = residual.shape[2]
    cols = teacher.shape[2]
    tensor_count = lax.axis_size("tensor")
    cand_count = lax.axis_size("cand")
    share = cand_rows // tensor_count
    near = cols // cand_rows
    tensor_index = lax.axis_index("tensor")
    dp_index = lax.axis_index("dp")
    cand_index = lax.axis_index("cand")

    full_weight = lax.all_gather(out_weight, "cand", axis=0, tiled=True)

    low_terms = jnp.einsum(
        "qch,hr->qcr", context, adapter_down, preferred_element_type=F32
    ).astype(BF16)
    low_all = lax.all_gather(low_terms, "tensor", axis=0)
    adapter_in = jnp.sum(low_all.astype(F32), axis=0).astype(BF16)
    adapter_own = lax.dynamic_slice_in_dim(adapter_in, tensor_index * share, share, 1)
    lifted = jnp.einsum("qcr,rd->qcd", adapter_own, adapter_up_weight, preferred_element_type=F32)
    base = residual.astype(F32) + ADAPTER_SCALE * lifted

    mask_count = jnp.sum(pair_mask.astype(F32), axis=(1, 2))
    pairs = gather_copies(jnp.stack([pair_mask.astype(BF16), teacher]), "tensor")
    valid = pairs[:, 0]
    known = valid.astype(F32) * pairs[:, 1].astype(F32)
    row_known = jnp.sum(known, axis=(0, 3))
    col_known = jnp.sum(known, axis=2)

    full_weight, adapter_in, base, mask_count, valid, row_known, col_known = (
        lax.optimization_barrier(
            (full_weight, adapter_in, base, mask_count, valid, row_known, col_known)
        )
    )

    by_owner = jnp.swapaxes(
        context.reshape(queries, tensor_count, share, context.shape[2]), 0, 1
    )
    head_terms = jnp.einsum(
        "tqch,dh->tqcd", by_owner, full_weight, preferred_element_type=F32
    ).astype(BF16)
    head_terms = lax.all_to_all(head_terms, "tensor", 0, 0, tiled=True)
    hidden = (base + jnp.sum(head_terms.astype(F32), axis=0)).astype(BF16).astype(F32)
    inv_rms = lax.rsqrt(jnp.mean(hidden * hidden, axis=2) + epsilon)
    gain = norm_gain * score_weight
    dot = jnp.sum(hidden * gain, axis=2)
    scores = dot * inv_rms
    slant = inv_rms * inv_rms * dot / width
    unit = inv_rms[:, :, None] * (gain - hidden * slant[:, :, None])

    unit_sent, unit, scores = lax.optimization_barrier((unit.astype(BF16), unit, scores))
    unit_all = lax.all_gather(unit_sent, "tensor", axis=1, tiled=True)
    message = jnp.concatenate(
        [scores, jnp.broadcast_to(mask_count[:, None], (queries, 128 - share))], axis=1
    )
    message = gather_copies(message, ("cand", "tensor"))
    count = jnp.sum(message[:, :, share], axis=0)
    message = message[:, :, :share].reshape(cand_count, tensor_count, queries, share)
    own_scores = lax.dynamic_index_in_dim(message, cand_index, 0, keepdims=False)
    own_scores = jnp.swapaxes(own_scores, 0, 1).reshape(queries, cand_rows)
    message = message.reshape(tensor_count, near, tensor_count, queries, share)
    col_scores = jnp.moveaxis(message, 3, 1).reshape(tensor_count, queries, cols)

    margin = own_scores[None, :, :, None] - col_scores[:, :, None, :]
    chance = valid.astype(F32) * jax.nn.sigmoid(margin)
    row_sum = jnp.sum(chance, axis=(0, 3)) - row_known
    columns = jnp.sum(chance, axis=2) - col_known
    columns = columns.reshape(tensor_count, queries, near, cand_rows)
    columns = jnp.swapaxes(columns, 1, 2).reshape(cand_count, queries, cand_rows)
    columns, row_sum, own_late, col_late = lax.optimization_barrier(
        (columns, row_sum, own_scores, col_scores)
    )
    columns = lax.all_to_all(columns, "cand", 0, 0, tiled=True)

    margin = own_late[None, :, :, None] - col_late[:, :, None, :]
    total = (
        jnp.sum(valid.astype(F32) * jax.nn.softplus(margin), axis=(0, 2, 3))
        - jnp.sum(own_late * row_known, axis=1)
        + jnp.sum(col_late * col_known, axis=(0, 2))
    )
    adapter_unit = ADAPTER_SCALE * jnp.einsum(
        "qcd,rd->qcr", unit_all, adapter_up_weight, preferred_element_type=F32
    )
    context_unit = jnp.einsum(
        "qcd,dh->qch", unit_all, full_weight, preferred_element_type=F32
    ) + jnp.einsum("qcr,hr->qch", adapter_unit.astype(BF16), adapter_down, preferred_element_type=F32)
    columns, total, adapter_unit, context_unit, count = lax.optimization_barrier(
        (columns, total, adapter_unit, context_unit, count)
    )
    score_grad = (row_sum - jnp.sum(columns, axis=0)) * (loss_scale / count)[:, None]

    own_grad = lax.dynamic_slice_in_dim(score_grad, tensor_index * share, share, 1)
    grad_rows = (own_grad[:, :, None] * unit).astype(BF16)

    context_grad = (score_grad[:, :, None] * context_unit).astype(BF16)
    adapter_back = (score_grad[:, :, None] * adapter_unit).astype(BF16)
    down_local = jnp.einsum("qcr,qch->rh", adapter_back, context, preferred_element_type=F32)
    block = lax.dynamic_slice_in_dim(
        unit_all, tensor_index * context.shape[2], context.shape[2], 2
    )
    block = (score_grad[:, :, None] * block.astype(F32)).astype(BF16)
    up_local = ADAPTER_SCALE * jnp.einsum(
        "qcr,qcd->rd", adapter_in, block, preferred_element_type=F32
    )

    slots = jnp.zeros((128,), F32)
    slots = lax.dynamic_update_slice_in_dim(slots, total, dp_index * queries, 0)
    flat = jnp.concatenate([down_local, up_local], axis=0)
    wide = flat.shape[1]
    flat = jnp.concatenate([flat, jnp.broadcast_to(slots, (flat.shape[0], 128))], axis=1)
    pieces = lax.all_to_all(flat, "cand", 0, 0, tiled=True)
    piece = jnp.sum(pieces.reshape(cand_count, -1, flat.shape[1]), axis=0)
    piece = lax.psum(piece, "dp")
    flat = gather_copies(piece[:, :wide], "cand").reshape(flat.shape[0], wide)
    rank = adapter_down.shape[1]
    down_grad = flat[:rank].T
    up_weight_gradient = flat[rank:]
    loss_sum = lax.dynamic_slice_in_dim(piece[0, wide:], dp_index * queries, queries, 0)
    pair_loss = loss_sum / count
    return (context_grad, grad_rows, down_grad, up_weight_gradient, pair_loss)


def solution(mesh):
    in_specs = (
        P("dp", "cand", "tensor"),
        P("dp", ("cand", "tensor"), None),
        P("cand", "tensor"),
        P("tensor", None),
        P(),
        P(),
        P(),
        P("dp", "cand", "tensor"),
        P("dp", "cand", "tensor"),
        P("dp"),
    )
    out_specs = (
        P("dp", "cand", "tensor"),
        P("dp", ("cand", "tensor"), None),
        P("tensor", None),
        P(None, "tensor"),
        P("dp"),
    )
    return jax.shard_map(
        on_device, mesh=mesh, in_specs=in_specs, out_specs=out_specs, check_vma=False
    )
```

```python
import jax
import jax.numpy as jnp
from jax import lax
from jax.sharding import PartitionSpec as P

ADAPTER_SCALE = 0.5
epsilon = 1e-06
F32 = jnp.float32
BF16 = jnp.bfloat16


def gather_copies(x, axis):
    copies = jnp.broadcast_to(x[None], (lax.axis_size(axis),) + x.shape)
    return lax.all_to_all(copies, axis, 0, 0, tiled=True)


def on_device(
    context,
    residual,
    out_weight,
    adapter_down,
    adapter_up_weight,
    norm_gain,
    score_weight,
    teacher,
    pair_mask,
    loss_scale,
):
    queries, cand_rows, _ = context.shape
    width = residual.shape[2]
    cols = teacher.shape[2]
    tensor_count = lax.axis_size("tensor")
    cand_count = lax.axis_size("cand")
    share = cand_rows // tensor_count
    near = cols // cand_rows
    tensor_index = lax.axis_index("tensor")
    dp_index = lax.axis_index("dp")
    cand_index = lax.axis_index("cand")
    dp_count = lax.axis_size("dp")

    full_weight = lax.all_gather(out_weight, "cand", axis=0, tiled=True)

    low_terms = jnp.einsum(
        "qch,hr->qcr", context, adapter_down, preferred_element_type=F32
    ).astype(BF16)
    low_all = lax.all_gather(low_terms, "tensor", axis=0)
    adapter_in = jnp.sum(low_all.astype(F32), axis=0).astype(BF16)
    adapter_own = lax.dynamic_slice_in_dim(adapter_in, tensor_index * share, share, 1)
    lifted = jnp.einsum("qcr,rd->qcd", adapter_own, adapter_up_weight, preferred_element_type=F32)
    base = residual.astype(F32) + ADAPTER_SCALE * lifted

    mask_count = jnp.sum(pair_mask.astype(F32), axis=(1, 2))
    pairs = gather_copies(jnp.stack([pair_mask.astype(BF16), teacher]), "tensor")
    valid = pairs[:, 0]
    known = valid.astype(F32) * pairs[:, 1].astype(F32)
    row_known = jnp.sum(known, axis=(0, 3))
    col_known = jnp.sum(known, axis=2)

    full_weight, adapter_in, base, mask_count, valid, row_known, col_known = (
        lax.optimization_barrier(
            (full_weight, adapter_in, base, mask_count, valid, row_known, col_known)
        )
    )

    by_owner = jnp.swapaxes(
        context.reshape(queries, tensor_count, share, context.shape[2]), 0, 1
    )
    head_terms = jnp.einsum(
        "tqch,dh->tqcd", by_owner, full_weight, preferred_element_type=F32
    ).astype(BF16)
    head_terms = lax.all_to_all(head_terms, "tensor", 0, 0, tiled=True)
    hidden = (base + jnp.sum(head_terms.astype(F32), axis=0)).astype(BF16).astype(F32)
    inv_rms = lax.rsqrt(jnp.mean(hidden * hidden, axis=2) + epsilon)
    gain = norm_gain * score_weight
    dot = jnp.sum(hidden * gain, axis=2)
    scores = dot * inv_rms
    slant = inv_rms * inv_rms * dot / width
    unit = inv_rms[:, :, None] * (gain - hidden * slant[:, :, None])

    unit_sent, unit, scores = lax.optimization_barrier((unit.astype(BF16), unit, scores))
    unit_all = lax.all_gather(unit_sent, "tensor", axis=1, tiled=True)
    message = jnp.concatenate(
        [scores, jnp.broadcast_to(mask_count[:, None], (queries, 128 - share))], axis=1
    )
    message = gather_copies(message, ("cand", "tensor"))
    count = jnp.sum(message[:, :, share], axis=0)
    message = message[:, :, :share].reshape(cand_count, tensor_count, queries, share)
    own_scores = lax.dynamic_index_in_dim(message, cand_index, 0, keepdims=False)
    own_scores = jnp.swapaxes(own_scores, 0, 1).reshape(queries, cand_rows)
    message = message.reshape(tensor_count, near, tensor_count, queries, share)
    col_scores = jnp.moveaxis(message, 3, 1).reshape(tensor_count, queries, cols)

    margin = own_scores[None, :, :, None] - col_scores[:, :, None, :]
    chance = valid.astype(F32) * jax.nn.sigmoid(margin)
    row_sum = jnp.sum(chance, axis=(0, 3)) - row_known
    columns = jnp.sum(chance, axis=2) - col_known
    columns = columns.reshape(tensor_count, queries, near, cand_rows)
    columns = jnp.swapaxes(columns, 1, 2).reshape(cand_count, queries, cand_rows)
    columns, row_sum, own_late, col_late = lax.optimization_barrier(
        (columns, row_sum, own_scores, col_scores)
    )
    columns = lax.all_to_all(columns, "cand", 0, 0, tiled=True)

    margin = own_late[None, :, :, None] - col_late[:, :, None, :]
    total = (
        jnp.sum(valid.astype(F32) * jax.nn.softplus(margin), axis=(0, 2, 3))
        - jnp.sum(own_late * row_known, axis=1)
        + jnp.sum(col_late * col_known, axis=(0, 2))
    )
    adapter_unit = ADAPTER_SCALE * jnp.einsum(
        "qcd,rd->qcr", unit_all, adapter_up_weight, preferred_element_type=F32
    )
    context_unit = jnp.einsum(
        "qcd,dh->qch", unit_all, full_weight, preferred_element_type=F32
    ) + jnp.einsum("qcr,hr->qch", adapter_unit.astype(BF16), adapter_down, preferred_element_type=F32)
    columns, total, adapter_unit, context_unit, count = lax.optimization_barrier(
        (columns, total, adapter_unit, context_unit, count)
    )
    score_grad = (row_sum - jnp.sum(columns, axis=0)) * (loss_scale / count)[:, None]

    own_grad = lax.dynamic_slice_in_dim(score_grad, tensor_index * share, share, 1)
    grad_rows = (own_grad[:, :, None] * unit).astype(BF16)

    context_grad = (score_grad[:, :, None] * context_unit).astype(BF16)
    adapter_back = (score_grad[:, :, None] * adapter_unit).astype(BF16)
    down_local = jnp.einsum("qcr,qch->rh", adapter_back, context, preferred_element_type=F32)
    block = lax.dynamic_slice_in_dim(
        unit_all, tensor_index * context.shape[2], context.shape[2], 2
    )
    block = (score_grad[:, :, None] * block.astype(F32)).astype(BF16)
    up_local = ADAPTER_SCALE * jnp.einsum(
        "qcr,qcd->rd", adapter_in, block, preferred_element_type=F32
    )

    rank = adapter_down.shape[1]
    flat = jnp.concatenate([down_local, up_local], axis=0)
    wide = flat.shape[1]
    segments = cand_count // near
    members = dp_count * near
    near_groups = [
        [d * cand_count + a * near + b for d in range(dp_count) for b in range(near)]
        for a in range(segments)
    ]
    far_groups = [[a * near + b for a in range(segments)] for b in range(near)]
    slots = lax.dynamic_update_slice_in_dim(
        jnp.zeros((1, 1, 128), F32), total[None, None, :], dp_index * queries, 2
    )
    tiles = flat.reshape(2 * rank // 8, 8, wide // 128, 128)
    tiles = jnp.swapaxes(tiles, 1, 2).reshape(-1, 8, 128)
    used = tiles.shape[0]
    height = -(-(used + 1) // members)
    slots = jnp.pad(slots, ((0, height * members - used - 1), (0, 7), (0, 0)))
    tiles = jnp.concatenate([tiles, slots]).reshape(members, 8 * height, 128)
    tiles = lax.all_to_all(
        tiles, ("dp", "cand"), 0, 0, axis_index_groups=near_groups, tiled=True
    )
    tiles = lax.psum(jnp.sum(tiles, axis=0), "cand", axis_index_groups=far_groups)
    tiles = jnp.broadcast_to(tiles[None], (members,) + tiles.shape)
    tiles = lax.all_to_all(
        tiles, ("dp", "cand"), 0, 0, axis_index_groups=near_groups, tiled=True
    ).reshape(-1, 8, 128)
    loss_sum = lax.dynamic_slice_in_dim(tiles[used, 0], dp_index * queries, queries, 0)
    pair_loss = loss_sum / count
    flat = tiles[:used].reshape(2 * rank // 8, wide // 128, 8, 128)
    flat = jnp.swapaxes(flat, 1, 2).reshape(2 * rank, wide)
    down_grad = flat[:rank].T
    up_weight_gradient = flat[rank:]
    return (context_grad, grad_rows, down_grad, up_weight_gradient, pair_loss)


def solution(mesh):
    in_specs = (
        P("dp", "cand", "tensor"),
        P("dp", ("cand", "tensor"), None),
        P("cand", "tensor"),
        P("tensor", None),
        P(),
        P(),
        P(),
        P("dp", "cand", "tensor"),
        P("dp", "cand", "tensor"),
        P("dp"),
    )
    out_specs = (
        P("dp", "cand", "tensor"),
        P("dp", ("cand", "tensor"), None),
        P("tensor", None),
        P(None, "tensor"),
        P("dp"),
    )
    return jax.shard_map(
        on_device, mesh=mesh, in_specs=in_specs, out_specs=out_specs, check_vma=False
    )
```

```python
import jax
import jax.numpy as jnp
from jax import lax
from jax.sharding import PartitionSpec as P

ADAPTER_SCALE = 0.5
epsilon = 1e-06
F32 = jnp.float32
BF16 = jnp.bfloat16


def gather_copies(x, axis):
    copies = jnp.broadcast_to(x[None], (lax.axis_size(axis),) + x.shape)
    return lax.all_to_all(copies, axis, 0, 0, tiled=True)


def on_device(
    context,
    residual,
    out_weight,
    adapter_down,
    adapter_up_weight,
    norm_gain,
    score_weight,
    teacher,
    pair_mask,
    loss_scale,
):
    queries, cand_rows, _ = context.shape
    width = residual.shape[2]
    cols = teacher.shape[2]
    tensor_count = lax.axis_size("tensor")
    cand_count = lax.axis_size("cand")
    share = cand_rows // tensor_count
    near = cols // cand_rows
    tensor_index = lax.axis_index("tensor")
    dp_index = lax.axis_index("dp")
    cand_index = lax.axis_index("cand")
    dp_count = lax.axis_size("dp")

    full_weight = lax.all_gather(out_weight, "cand", axis=0, tiled=True)

    low_terms = jnp.einsum(
        "qch,hr->qcr", context, adapter_down, preferred_element_type=F32
    ).astype(BF16)
    low_all = lax.all_gather(low_terms, "tensor", axis=0)
    adapter_in = jnp.sum(low_all.astype(F32), axis=0).astype(BF16)
    adapter_own = lax.dynamic_slice_in_dim(adapter_in, tensor_index * share, share, 1)
    lifted = jnp.einsum("qcr,rd->qcd", adapter_own, adapter_up_weight, preferred_element_type=F32)
    base = residual.astype(F32) + ADAPTER_SCALE * lifted

    mask_count = jnp.sum(pair_mask.astype(F32), axis=(1, 2))
    pairs = gather_copies(jnp.stack([pair_mask.astype(BF16), teacher]), "tensor")
    valid = pairs[:, 0]
    known = valid.astype(F32) * pairs[:, 1].astype(F32)
    row_known = jnp.sum(known, axis=(0, 3))
    col_known = jnp.sum(known, axis=2)

    full_weight, adapter_in, base, mask_count, valid, row_known, col_known = (
        lax.optimization_barrier(
            (full_weight, adapter_in, base, mask_count, valid, row_known, col_known)
        )
    )

    by_owner = jnp.swapaxes(
        context.reshape(queries, tensor_count, share, context.shape[2]), 0, 1
    )
    half = width // 2
    head_first = jnp.einsum(
        "tqch,dh->tqcd", by_owner, full_weight[:half], preferred_element_type=F32
    ).astype(BF16)
    head_first = lax.all_to_all(head_first, "tensor", 0, 0, tiled=True)
    head_second = jnp.einsum(
        "tqch,dh->tqcd", by_owner, full_weight[half:], preferred_element_type=F32
    ).astype(BF16)
    head_first, head_second = lax.optimization_barrier((head_first, head_second))
    head_second = lax.all_to_all(head_second, "tensor", 0, 0, tiled=True)
    head_sum = jnp.concatenate(
        [jnp.sum(head_first.astype(F32), axis=0), jnp.sum(head_second.astype(F32), axis=0)], axis=2
    )
    hidden = (base + head_sum).astype(BF16).astype(F32)
    inv_rms = lax.rsqrt(jnp.mean(hidden * hidden, axis=2) + epsilon)
    gain = norm_gain * score_weight
    dot = jnp.sum(hidden * gain, axis=2)
    scores = dot * inv_rms
    slant = inv_rms * inv_rms * dot / width
    unit = inv_rms[:, :, None] * (gain - hidden * slant[:, :, None])

    unit_sent, unit, scores = lax.optimization_barrier((unit.astype(BF16), unit, scores))
    unit_all = lax.all_gather(unit_sent, "tensor", axis=1, tiled=True)
    message = jnp.concatenate(
        [scores, jnp.broadcast_to(mask_count[:, None], (queries, 128 - share))], axis=1
    )
    message = gather_copies(message, ("cand", "tensor"))
    count = jnp.sum(message[:, :, share], axis=0)
    message = message[:, :, :share].reshape(cand_count, tensor_count, queries, share)
    own_scores = lax.dynamic_index_in_dim(message, cand_index, 0, keepdims=False)
    own_scores = jnp.swapaxes(own_scores, 0, 1).reshape(queries, cand_rows)
    message = message.reshape(tensor_count, near, tensor_count, queries, share)
    col_scores = jnp.moveaxis(message, 3, 1).reshape(tensor_count, queries, cols)

    margin = own_scores[None, :, :, None] - col_scores[:, :, None, :]
    chance = valid.astype(F32) * jax.nn.sigmoid(margin)
    row_sum = jnp.sum(chance, axis=(0, 3)) - row_known
    columns = jnp.sum(chance, axis=2) - col_known
    columns = columns.reshape(tensor_count, queries, near, cand_rows)
    columns = jnp.swapaxes(columns, 1, 2).reshape(cand_count, queries, cand_rows)
    columns, row_sum, own_late, col_late = lax.optimization_barrier(
        (columns, row_sum, own_scores, col_scores)
    )
    columns = lax.all_to_all(columns, "cand", 0, 0, tiled=True)

    margin = own_late[None, :, :, None] - col_late[:, :, None, :]
    total = (
        jnp.sum(valid.astype(F32) * jax.nn.softplus(margin), axis=(0, 2, 3))
        - jnp.sum(own_late * row_known, axis=1)
        + jnp.sum(col_late * col_known, axis=(0, 2))
    )
    adapter_unit = ADAPTER_SCALE * jnp.einsum(
        "qcd,rd->qcr", unit_all, adapter_up_weight, preferred_element_type=F32
    )
    context_unit = jnp.einsum(
        "qcd,dh->qch", unit_all, full_weight, preferred_element_type=F32
    ) + jnp.einsum("qcr,hr->qch", adapter_unit.astype(BF16), adapter_down, preferred_element_type=F32)
    unit_block = lax.dynamic_slice_in_dim(
        unit_all, tensor_index * context.shape[2], context.shape[2], 2
    )
    columns, total, adapter_unit, context_unit, unit_block, count = lax.optimization_barrier(
        (columns, total, adapter_unit, context_unit, unit_block, count)
    )
    score_grad = (row_sum - jnp.sum(columns, axis=0)) * (loss_scale / count)[:, None]

    own_grad = lax.dynamic_slice_in_dim(score_grad, tensor_index * share, share, 1)
    grad_rows = (own_grad[:, :, None] * unit).astype(BF16)

    context_grad = (score_grad[:, :, None] * context_unit).astype(BF16)
    adapter_back = (score_grad[:, :, None] * adapter_unit).astype(BF16)
    down_local = jnp.einsum("qcr,qch->rh", adapter_back, context, preferred_element_type=F32)
    adapter_scaled = (score_grad[:, :, None] * adapter_in.astype(F32)).astype(BF16)
    up_local = ADAPTER_SCALE * jnp.einsum(
        "qcr,qcd->rd", adapter_scaled, unit_block, preferred_element_type=F32
    )

    rank = adapter_down.shape[1]
    flat = jnp.concatenate([down_local, up_local], axis=0)
    wide = flat.shape[1]
    segments = cand_count // near
    members = dp_count * near
    near_groups = [
        [d * cand_count + a * near + b for d in range(dp_count) for b in range(near)]
        for a in range(segments)
    ]
    far_groups = [[a * near + b for a in range(segments)] for b in range(near)]
    slots = lax.dynamic_update_slice_in_dim(
        jnp.zeros((1, 1, 128), F32), total[None, None, :], dp_index * queries, 2
    )
    tiles = flat.reshape(2 * rank // 8, 8, wide // 128, 128)
    tiles = jnp.swapaxes(tiles, 1, 2).reshape(-1, 8, 128)
    used = tiles.shape[0]
    height = -(-(used + 1) // members)
    slots = jnp.pad(slots, ((0, height * members - used - 1), (0, 7), (0, 0)))
    tiles = jnp.concatenate([tiles, slots]).reshape(members, 8 * height, 128)
    tiles = lax.all_to_all(
        tiles, ("dp", "cand"), 0, 0, axis_index_groups=near_groups, tiled=True
    )
    tiles = lax.psum(jnp.sum(tiles, axis=0), "cand", axis_index_groups=far_groups)
    tiles = jnp.broadcast_to(tiles[None], (members,) + tiles.shape)
    tiles = lax.all_to_all(
        tiles, ("dp", "cand"), 0, 0, axis_index_groups=near_groups, tiled=True
    ).reshape(-1, 8, 128)
    loss_sum = lax.dynamic_slice_in_dim(tiles[used, 0], dp_index * queries, queries, 0)
    pair_loss = loss_sum / count
    flat = tiles[:used].reshape(2 * rank // 8, wide // 128, 8, 128)
    flat = jnp.swapaxes(flat, 1, 2).reshape(2 * rank, wide)
    down_grad = flat[:rank].T
    up_weight_gradient = flat[rank:]
    return (context_grad, grad_rows, down_grad, up_weight_gradient, pair_loss)


def solution(mesh):
    in_specs = (
        P("dp", "cand", "tensor"),
        P("dp", ("cand", "tensor"), None),
        P("cand", "tensor"),
        P("tensor", None),
        P(),
        P(),
        P(),
        P("dp", "cand", "tensor"),
        P("dp", "cand", "tensor"),
        P("dp"),
    )
    out_specs = (
        P("dp", "cand", "tensor"),
        P("dp", ("cand", "tensor"), None),
        P("tensor", None),
        P(None, "tensor"),
        P("dp"),
    )
    return jax.shard_map(
        on_device, mesh=mesh, in_specs=in_specs, out_specs=out_specs, check_vma=False
    )
```

```python
import jax
import jax.numpy as jnp
from jax import lax
from jax.sharding import PartitionSpec as P

ADAPTER_SCALE = 0.5
epsilon = 1e-06
F32 = jnp.float32
BF16 = jnp.bfloat16


def gather_copies(x, axis):
    copies = jnp.broadcast_to(x[None], (lax.axis_size(axis),) + x.shape)
    return lax.all_to_all(copies, axis, 0, 0, tiled=True)


def on_device(
    context,
    residual,
    out_weight,
    adapter_down,
    adapter_up_weight,
    norm_gain,
    score_weight,
    teacher,
    pair_mask,
    loss_scale,
):
    queries, cand_rows, _ = context.shape
    width = residual.shape[2]
    cols = teacher.shape[2]
    tensor_count = lax.axis_size("tensor")
    cand_count = lax.axis_size("cand")
    share = cand_rows // tensor_count
    near = cols // cand_rows
    tensor_index = lax.axis_index("tensor")
    dp_index = lax.axis_index("dp")
    cand_index = lax.axis_index("cand")
    dp_count = lax.axis_size("dp")

    full_weight = lax.all_gather(out_weight, "cand", axis=0, tiled=True)

    low_terms = jnp.einsum(
        "qch,hr->qcr", context, adapter_down, preferred_element_type=F32
    ).astype(BF16)
    low_all = lax.all_gather(low_terms, "tensor", axis=0)
    adapter_in = jnp.sum(low_all.astype(F32), axis=0).astype(BF16)
    adapter_own = lax.dynamic_slice_in_dim(adapter_in, tensor_index * share, share, 1)
    lifted = jnp.einsum("qcr,rd->qcd", adapter_own, adapter_up_weight, preferred_element_type=F32)
    base = residual.astype(F32) + ADAPTER_SCALE * lifted

    mask_count = jnp.sum(pair_mask.astype(F32), axis=(1, 2))
    pairs = gather_copies(jnp.stack([pair_mask.astype(BF16), teacher]), "tensor")
    valid = pairs[:, 0]
    known = valid.astype(F32) * pairs[:, 1].astype(F32)
    row_known = jnp.sum(known, axis=(0, 3))
    col_known = jnp.sum(known, axis=2)

    full_weight, adapter_in, base, mask_count, valid, row_known, col_known = (
        lax.optimization_barrier(
            (full_weight, adapter_in, base, mask_count, valid, row_known, col_known)
        )
    )

    by_owner = jnp.swapaxes(
        context.reshape(queries, tensor_count, share, context.shape[2]), 0, 1
    )
    head_terms = jnp.einsum(
        "tqch,dh->tqcd", by_owner, full_weight, preferred_element_type=F32
    ).astype(BF16)
    head_terms = lax.all_to_all(head_terms, "tensor", 0, 0, tiled=True)
    head_sum = jnp.sum(head_terms.astype(F32), axis=0)
    hidden = (base + head_sum).astype(BF16).astype(F32)
    inv_rms = lax.rsqrt(jnp.mean(hidden * hidden, axis=2) + epsilon)
    gain = norm_gain * score_weight
    dot = jnp.sum(hidden * gain, axis=2)
    scores = dot * inv_rms
    slant = inv_rms * inv_rms * dot / width
    unit = inv_rms[:, :, None] * (gain - hidden * slant[:, :, None])

    message = jnp.concatenate(
        [scores, jnp.broadcast_to(mask_count[:, None], (queries, 128 - share))], axis=1
    )
    message = gather_copies(message, "tensor")
    count = jnp.sum(message[:, :, share], axis=0)
    own_scores = jnp.swapaxes(message[:, :, :share], 0, 1).reshape(queries, cand_rows)
    own_scores, count, unit_sent = lax.optimization_barrier((own_scores, count, unit.astype(BF16)))
    unit_all = lax.all_gather(unit_sent, "tensor", axis=1, tiled=True)
    counts = jnp.pad(count[None], ((0, 0), (0, cand_rows - queries)))
    message = gather_copies(jnp.concatenate([own_scores, counts], axis=0), "cand")
    count = jnp.sum(message[:, queries, :queries], axis=0)
    message = message[:, :queries].reshape(tensor_count, near, queries, cand_rows)
    col_scores = jnp.swapaxes(message, 1, 2).reshape(tensor_count, queries, cols)

    margin = own_scores[None, :, :, None] - col_scores[:, :, None, :]
    chance = valid.astype(F32) * jax.nn.sigmoid(margin)
    row_sum = jnp.sum(chance, axis=(0, 3)) - row_known
    columns = jnp.sum(chance, axis=2) - col_known
    columns = columns.reshape(tensor_count, queries, near, cand_rows)
    columns = jnp.swapaxes(columns, 1, 2).reshape(cand_count, queries, cand_rows)
    columns, row_sum, own_late, col_late = lax.optimization_barrier(
        (columns, row_sum, own_scores, col_scores)
    )
    columns = lax.all_to_all(columns, "cand", 0, 0, tiled=True)

    margin = own_late[None, :, :, None] - col_late[:, :, None, :]
    total = (
        jnp.sum(valid.astype(F32) * jax.nn.softplus(margin), axis=(0, 2, 3))
        - jnp.sum(own_late * row_known, axis=1)
        + jnp.sum(col_late * col_known, axis=(0, 2))
    )
    adapter_unit = ADAPTER_SCALE * jnp.einsum(
        "qcd,rd->qcr", unit_all, adapter_up_weight, preferred_element_type=F32
    )
    context_unit = jnp.einsum(
        "qcd,dh->qch", unit_all, full_weight, preferred_element_type=F32
    ) + jnp.einsum("qcr,hr->qch", adapter_unit.astype(BF16), adapter_down, preferred_element_type=F32)
    unit_block = lax.dynamic_slice_in_dim(
        unit_all, tensor_index * context.shape[2], context.shape[2], 2
    )
    columns, total, adapter_unit, unit_block = lax.optimization_barrier(
        (columns, total, adapter_unit, unit_block)
    )
    score_grad = (row_sum - jnp.sum(columns, axis=0)) * (loss_scale / count)[:, None]

    own_grad = lax.dynamic_slice_in_dim(score_grad, tensor_index * share, share, 1)
    grad_rows = (own_grad[:, :, None] * unit).astype(BF16)

    context_grad = (score_grad[:, :, None] * context_unit).astype(BF16)
    adapter_back = (score_grad[:, :, None] * adapter_unit).astype(BF16)
    down_local = jnp.einsum("qcr,qch->rh", adapter_back, context, preferred_element_type=F32)
    adapter_scaled = (score_grad[:, :, None] * adapter_in.astype(F32)).astype(BF16)
    up_local = ADAPTER_SCALE * jnp.einsum(
        "qcr,qcd->rd", adapter_scaled, unit_block, preferred_element_type=F32
    )

    rank = adapter_down.shape[1]
    flat = jnp.concatenate([down_local, up_local], axis=0)
    wide = flat.shape[1]
    segments = cand_count // near
    members = dp_count * near
    near_groups = [
        [d * cand_count + a * near + b for d in range(dp_count) for b in range(near)]
        for a in range(segments)
    ]
    far_groups = [[a * near + b for a in range(segments)] for b in range(near)]
    slots = lax.dynamic_update_slice_in_dim(
        jnp.zeros((1, 1, 128), F32), total[None, None, :], dp_index * queries, 2
    )
    tiles = flat.reshape(2 * rank // 8, 8, wide // 128, 128)
    tiles = jnp.swapaxes(tiles, 1, 2).reshape(-1, 8, 128)
    used = tiles.shape[0]
    height = -(-(used + 1) // members)
    slots = jnp.pad(slots, ((0, height * members - used - 1), (0, 7), (0, 0)))
    tiles = jnp.concatenate([tiles, slots]).reshape(members, 8 * height, 128)
    tiles = lax.all_to_all(
        tiles, ("dp", "cand"), 0, 0, axis_index_groups=near_groups, tiled=True
    )
    tiles = lax.psum(jnp.sum(tiles, axis=0), "cand", axis_index_groups=far_groups)
    tiles = jnp.broadcast_to(tiles[None], (members,) + tiles.shape)
    tiles = lax.all_to_all(
        tiles, ("dp", "cand"), 0, 0, axis_index_groups=near_groups, tiled=True
    ).reshape(-1, 8, 128)
    loss_sum = lax.dynamic_slice_in_dim(tiles[used, 0], dp_index * queries, queries, 0)
    pair_loss = loss_sum / count
    flat = tiles[:used].reshape(2 * rank // 8, wide // 128, 8, 128)
    flat = jnp.swapaxes(flat, 1, 2).reshape(2 * rank, wide)
    down_grad = flat[:rank].T
    up_weight_gradient = flat[rank:]
    return (context_grad, grad_rows, down_grad, up_weight_gradient, pair_loss)


def solution(mesh):
    in_specs = (
        P("dp", "cand", "tensor"),
        P("dp", ("cand", "tensor"), None),
        P("cand", "tensor"),
        P("tensor", None),
        P(),
        P(),
        P(),
        P("dp", "cand", "tensor"),
        P("dp", "cand", "tensor"),
        P("dp"),
    )
    out_specs = (
        P("dp", "cand", "tensor"),
        P("dp", ("cand", "tensor"), None),
        P("tensor", None),
        P(None, "tensor"),
        P("dp"),
    )
    return jax.shard_map(
        on_device, mesh=mesh, in_specs=in_specs, out_specs=out_specs, check_vma=False
    )
```

```python
import jax
import jax.numpy as jnp
from jax import lax
from jax.sharding import PartitionSpec as P

ADAPTER_SCALE = 0.5
epsilon = 1e-06
F32 = jnp.float32
BF16 = jnp.bfloat16


def gather_copies(x, axis):
    copies = jnp.broadcast_to(x[None], (lax.axis_size(axis),) + x.shape)
    return lax.all_to_all(copies, axis, 0, 0, tiled=True)


def on_device(
    context,
    residual,
    out_weight,
    adapter_down,
    adapter_up_weight,
    norm_gain,
    score_weight,
    teacher,
    pair_mask,
    loss_scale,
):
    queries, cand_rows, _ = context.shape
    width = residual.shape[2]
    cols = teacher.shape[2]
    tensor_count = lax.axis_size("tensor")
    cand_count = lax.axis_size("cand")
    share = cand_rows // tensor_count
    near = cols // cand_rows
    tensor_index = lax.axis_index("tensor")
    dp_index = lax.axis_index("dp")
    cand_index = lax.axis_index("cand")
    dp_count = lax.axis_size("dp")

    full_weight = lax.all_gather(out_weight, "cand", axis=0, tiled=True)

    low_terms = jnp.einsum(
        "qch,hr->qcr", context, adapter_down, preferred_element_type=F32
    ).astype(BF16)
    low_all = lax.all_gather(low_terms, "tensor", axis=0)
    adapter_in = jnp.sum(low_all.astype(F32), axis=0).astype(BF16)
    adapter_own = lax.dynamic_slice_in_dim(adapter_in, tensor_index * share, share, 1)
    lifted = jnp.einsum("qcr,rd->qcd", adapter_own, adapter_up_weight, preferred_element_type=F32)
    base = residual.astype(F32) + ADAPTER_SCALE * lifted

    mask_count = jnp.sum(pair_mask.astype(F32), axis=(1, 2))
    pairs = gather_copies(jnp.stack([pair_mask.astype(BF16), teacher]), "tensor")
    known = pairs[:, 0].astype(F32) * pairs[:, 1].astype(F32)
    row_known = jnp.sum(known, axis=(0, 3))
    col_known = jnp.sum(known, axis=2)

    full_weight, adapter_in, base, mask_count, pairs, row_known, col_known = (
        lax.optimization_barrier(
            (full_weight, adapter_in, base, mask_count, pairs, row_known, col_known)
        )
    )
    valid = pairs[:, 0]

    by_owner = jnp.swapaxes(
        context.reshape(queries, tensor_count, share, context.shape[2]), 0, 1
    )
    head_terms = jnp.einsum(
        "tqch,dh->tqcd", by_owner, full_weight, preferred_element_type=F32
    ).astype(BF16)
    head_terms = lax.all_to_all(head_terms, "tensor", 0, 0, tiled=True)
    hidden = (base + jnp.sum(head_terms.astype(F32), axis=0)).astype(BF16).astype(F32)
    inv_rms = lax.rsqrt(jnp.mean(hidden * hidden, axis=2) + epsilon)
    gain = norm_gain * score_weight
    dot = jnp.sum(hidden * gain, axis=2)
    scores = dot * inv_rms
    slant = inv_rms * inv_rms * dot / width
    unit = inv_rms[:, :, None] * (gain - hidden * slant[:, :, None])

    unit_sent, unit, scores = lax.optimization_barrier((unit.astype(BF16), unit, scores))
    unit_all = lax.all_gather(unit_sent, "tensor", axis=1, tiled=True)
    message = jnp.concatenate(
        [scores, jnp.broadcast_to(mask_count[:, None], (queries, 128 - share))], axis=1
    )
    message = gather_copies(message, ("cand", "tensor"))
    count = jnp.sum(message[:, :, share], axis=0)
    message = message[:, :, :share].reshape(cand_count, tensor_count, queries, share)
    own_scores = lax.dynamic_index_in_dim(message, cand_index, 0, keepdims=False)
    own_scores = jnp.swapaxes(own_scores, 0, 1).reshape(queries, cand_rows)
    message = message.reshape(tensor_count, near, tensor_count, queries, share)
    col_scores = jnp.moveaxis(message, 3, 1).reshape(tensor_count, queries, cols)

    margin = own_scores[None, :, :, None] - col_scores[:, :, None, :]
    chance = valid.astype(F32) * jax.nn.sigmoid(margin)
    row_sum = jnp.sum(chance, axis=(0, 3)) - row_known
    columns = jnp.sum(chance, axis=2) - col_known
    columns = columns.reshape(tensor_count, queries, near, cand_rows)
    columns = jnp.swapaxes(columns, 1, 2).reshape(cand_count, queries, cand_rows)
    columns, row_sum, own_late, col_late = lax.optimization_barrier(
        (columns, row_sum, own_scores, col_scores)
    )
    columns = lax.all_to_all(columns, "cand", 0, 0, tiled=True)

    margin = own_late[None, :, :, None] - col_late[:, :, None, :]
    total = (
        jnp.sum(valid.astype(F32) * jax.nn.softplus(margin), axis=(0, 2, 3))
        - jnp.sum(own_late * row_known, axis=1)
        + jnp.sum(col_late * col_known, axis=(0, 2))
    )
    adapter_unit = ADAPTER_SCALE * jnp.einsum(
        "qcd,rd->qcr", unit_all, adapter_up_weight, preferred_element_type=F32
    )
    context_unit = jnp.einsum(
        "qcd,dh->qch", unit_all, full_weight, preferred_element_type=F32
    ) + jnp.einsum("qcr,hr->qch", adapter_unit.astype(BF16), adapter_down, preferred_element_type=F32)
    unit_block = lax.dynamic_slice_in_dim(
        unit_all, tensor_index * context.shape[2], context.shape[2], 2
    )
    columns, total, adapter_unit, context_unit, unit_block, count = lax.optimization_barrier(
        (columns, total, adapter_unit, context_unit, unit_block, count)
    )
    score_grad = (row_sum - jnp.sum(columns, axis=0)) * (loss_scale / count)[:, None]

    own_grad = lax.dynamic_slice_in_dim(score_grad, tensor_index * share, share, 1)
    grad_rows = (own_grad[:, :, None] * unit).astype(BF16)

    context_grad = (score_grad[:, :, None] * context_unit).astype(BF16)
    adapter_back = (score_grad[:, :, None] * adapter_unit).astype(BF16)
    down_local = jnp.einsum("qcr,qch->rh", adapter_back, context, preferred_element_type=F32)
    adapter_scaled = (score_grad[:, :, None] * adapter_in.astype(F32)).astype(BF16)
    up_local = ADAPTER_SCALE * jnp.einsum(
        "qcr,qcd->rd", adapter_scaled, unit_block, preferred_element_type=F32
    )

    rank = adapter_down.shape[1]
    flat = jnp.concatenate([down_local, up_local], axis=0)
    wide = flat.shape[1]
    segments = cand_count // near
    members = dp_count * near
    near_groups = [
        [d * cand_count + a * near + b for d in range(dp_count) for b in range(near)]
        for a in range(segments)
    ]
    far_groups = [[a * near + b for a in range(segments)] for b in range(near)]
    slots = lax.dynamic_update_slice_in_dim(
        jnp.zeros((1, 1, 128), F32), total[None, None, :], dp_index * queries, 2
    )
    tiles = flat.reshape(2 * rank // 8, 8, wide // 128, 128)
    tiles = jnp.swapaxes(tiles, 1, 2).reshape(-1, 8, 128)
    used = tiles.shape[0]
    height = -(-(used + 1) // members)
    slots = jnp.pad(slots, ((0, height * members - used - 1), (0, 7), (0, 0)))
    tiles = jnp.concatenate([tiles, slots]).reshape(members, 8 * height, 128)
    tiles = lax.all_to_all(
        tiles, ("dp", "cand"), 0, 0, axis_index_groups=near_groups, tiled=True
    )
    tiles = lax.psum(jnp.sum(tiles, axis=0), "cand", axis_index_groups=far_groups)
    tiles = jnp.broadcast_to(tiles[None], (members,) + tiles.shape)
    tiles = lax.all_to_all(
        tiles, ("dp", "cand"), 0, 0, axis_index_groups=near_groups, tiled=True
    ).reshape(-1, 8, 128)
    loss_sum = lax.dynamic_slice_in_dim(tiles[used, 0], dp_index * queries, queries, 0)
    pair_loss = loss_sum / count
    flat = tiles[:used].reshape(2 * rank // 8, wide // 128, 8, 128)
    flat = jnp.swapaxes(flat, 1, 2).reshape(2 * rank, wide)
    down_grad = flat[:rank].T
    up_weight_gradient = flat[rank:]
    return (context_grad, grad_rows, down_grad, up_weight_gradient, pair_loss)


def solution(mesh):
    in_specs = (
        P("dp", "cand", "tensor"),
        P("dp", ("cand", "tensor"), None),
        P("cand", "tensor"),
        P("tensor", None),
        P(),
        P(),
        P(),
        P("dp", "cand", "tensor"),
        P("dp", "cand", "tensor"),
        P("dp"),
    )
    out_specs = (
        P("dp", "cand", "tensor"),
        P("dp", ("cand", "tensor"), None),
        P("tensor", None),
        P(None, "tensor"),
        P("dp"),
    )
    return jax.shard_map(
        on_device, mesh=mesh, in_specs=in_specs, out_specs=out_specs, check_vma=False
    )
```

```python
import jax
import jax.numpy as jnp
from jax import lax
from jax.sharding import PartitionSpec as P

ADAPTER_SCALE = 0.5
epsilon = 1e-06
F32 = jnp.float32
BF16 = jnp.bfloat16


def gather_copies(x, axis):
    copies = jnp.broadcast_to(x[None], (lax.axis_size(axis),) + x.shape)
    return lax.all_to_all(copies, axis, 0, 0, tiled=True)


def on_device(
    context,
    residual,
    out_weight,
    adapter_down,
    adapter_up_weight,
    norm_gain,
    score_weight,
    teacher,
    pair_mask,
    loss_scale,
):
    queries, cand_rows, _ = context.shape
    width = residual.shape[2]
    cols = teacher.shape[2]
    tensor_count = lax.axis_size("tensor")
    cand_count = lax.axis_size("cand")
    share = cand_rows // tensor_count
    near = cols // cand_rows
    tensor_index = lax.axis_index("tensor")
    dp_index = lax.axis_index("dp")
    cand_index = lax.axis_index("cand")
    dp_count = lax.axis_size("dp")

    full_weight = lax.all_gather(out_weight, "cand", axis=0, tiled=True)

    low_terms = jnp.einsum(
        "qch,hr->qcr", context, adapter_down, preferred_element_type=F32
    ).astype(BF16)
    low_all = lax.all_gather(low_terms, "tensor", axis=0)
    adapter_in = jnp.sum(low_all.astype(F32), axis=0).astype(BF16)
    adapter_own = lax.dynamic_slice_in_dim(adapter_in, tensor_index * share, share, 1)
    lifted = jnp.einsum("qcr,rd->qcd", adapter_own, adapter_up_weight, preferred_element_type=F32)
    base = residual.astype(F32) + ADAPTER_SCALE * lifted

    mask_count = jnp.sum(pair_mask.astype(F32), axis=(1, 2))
    pairs = gather_copies(jnp.stack([pair_mask.astype(BF16), teacher]), "tensor")
    known = pairs[:, 0].astype(F32) * pairs[:, 1].astype(F32)
    row_known = jnp.sum(known, axis=(0, 3))
    col_known = jnp.sum(known, axis=2)

    full_weight, adapter_in, base, mask_count, pairs, row_known, col_known = (
        lax.optimization_barrier(
            (full_weight, adapter_in, base, mask_count, pairs, row_known, col_known)
        )
    )

    by_owner = jnp.swapaxes(
        context.reshape(queries, tensor_count, share, context.shape[2]), 0, 1
    )
    head_terms = jnp.einsum(
        "tqch,dh->tqcd", by_owner, full_weight, preferred_element_type=F32
    ).astype(BF16)
    head_terms = lax.all_to_all(head_terms, "tensor", 0, 0, tiled=True)
    hidden = (base + jnp.sum(head_terms.astype(F32), axis=0)).astype(BF16).astype(F32)
    inv_rms = lax.rsqrt(jnp.mean(hidden * hidden, axis=2) + epsilon)
    gain = norm_gain * score_weight
    dot = jnp.sum(hidden * gain, axis=2)
    scores = dot * inv_rms
    slant = inv_rms * inv_rms * dot / width
    unit = inv_rms[:, :, None] * (gain - hidden * slant[:, :, None])

    pairs, scores = lax.optimization_barrier((pairs, scores))
    valid = lax.optimization_barrier(pairs[:, 0])

    unit_sent, unit, scores = lax.optimization_barrier((unit.astype(BF16), unit, scores))
    unit_all = lax.all_gather(unit_sent, "tensor", axis=1, tiled=True)
    message = jnp.concatenate(
        [scores, jnp.broadcast_to(mask_count[:, None], (queries, 128 - share))], axis=1
    )
    message = gather_copies(message, ("cand", "tensor"))
    count = jnp.sum(message[:, :, share], axis=0)
    message = message[:, :, :share].reshape(cand_count, tensor_count, queries, share)
    own_scores = lax.dynamic_index_in_dim(message, cand_index, 0, keepdims=False)
    own_scores = jnp.swapaxes(own_scores, 0, 1).reshape(queries, cand_rows)
    message = message.reshape(tensor_count, near, tensor_count, queries, share)
    col_scores = jnp.moveaxis(message, 3, 1).reshape(tensor_count, queries, cols)

    margin = own_scores[None, :, :, None] - col_scores[:, :, None, :]
    chance = valid.astype(F32) * jax.nn.sigmoid(margin)
    row_sum = jnp.sum(chance, axis=(0, 3)) - row_known
    columns = jnp.sum(chance, axis=2) - col_known
    columns = columns.reshape(tensor_count, queries, near, cand_rows)
    columns = jnp.swapaxes(columns, 1, 2).reshape(cand_count, queries, cand_rows)
    columns, row_sum, own_late, col_late = lax.optimization_barrier(
        (columns, row_sum, own_scores, col_scores)
    )
    columns = lax.all_to_all(columns, "cand", 0, 0, tiled=True)

    margin = own_late[None, :, :, None] - col_late[:, :, None, :]
    total = (
        jnp.sum(valid.astype(F32) * jax.nn.softplus(margin), axis=(0, 2, 3))
        - jnp.sum(own_late * row_known, axis=1)
        + jnp.sum(col_late * col_known, axis=(0, 2))
    )
    adapter_unit = ADAPTER_SCALE * jnp.einsum(
        "qcd,rd->qcr", unit_all, adapter_up_weight, preferred_element_type=F32
    )
    context_unit = jnp.einsum(
        "qcd,dh->qch", unit_all, full_weight, preferred_element_type=F32
    ) + jnp.einsum("qcr,hr->qch", adapter_unit.astype(BF16), adapter_down, preferred_element_type=F32)
    unit_block = lax.dynamic_slice_in_dim(
        unit_all, tensor_index * context.shape[2], context.shape[2], 2
    )
    columns, total, adapter_unit, context_unit, unit_block, count = lax.optimization_barrier(
        (columns, total, adapter_unit, context_unit, unit_block, count)
    )
    score_grad = (row_sum - jnp.sum(columns, axis=0)) * (loss_scale / count)[:, None]

    own_grad = lax.dynamic_slice_in_dim(score_grad, tensor_index * share, share, 1)
    grad_rows = (own_grad[:, :, None] * unit).astype(BF16)

    context_grad = (score_grad[:, :, None] * context_unit).astype(BF16)
    adapter_back = (score_grad[:, :, None] * adapter_unit).astype(BF16)
    down_local = jnp.einsum("qcr,qch->rh", adapter_back, context, preferred_element_type=F32)
    adapter_scaled = (score_grad[:, :, None] * adapter_in.astype(F32)).astype(BF16)
    up_local = ADAPTER_SCALE * jnp.einsum(
        "qcr,qcd->rd", adapter_scaled, unit_block, preferred_element_type=F32
    )

    rank = adapter_down.shape[1]
    flat = jnp.concatenate([down_local, up_local], axis=0)
    wide = flat.shape[1]
    segments = cand_count // near
    members = dp_count * near
    near_groups = [
        [d * cand_count + a * near + b for d in range(dp_count) for b in range(near)]
        for a in range(segments)
    ]
    far_groups = [[a * near + b for a in range(segments)] for b in range(near)]
    slots = lax.dynamic_update_slice_in_dim(
        jnp.zeros((1, 1, 128), F32), total[None, None, :], dp_index * queries, 2
    )
    tiles = flat.reshape(2 * rank // 8, 8, wide // 128, 128)
    tiles = jnp.swapaxes(tiles, 1, 2).reshape(-1, 8, 128)
    used = tiles.shape[0]
    height = -(-(used + 1) // members)
    slots = jnp.pad(slots, ((0, height * members - used - 1), (0, 7), (0, 0)))
    tiles = jnp.concatenate([tiles, slots]).reshape(members, 8 * height, 128)
    tiles = lax.all_to_all(
        tiles, ("dp", "cand"), 0, 0, axis_index_groups=near_groups, tiled=True
    )
    tiles = lax.psum(jnp.sum(tiles, axis=0), "cand", axis_index_groups=far_groups)
    tiles = jnp.broadcast_to(tiles[None], (members,) + tiles.shape)
    tiles = lax.all_to_all(
        tiles, ("dp", "cand"), 0, 0, axis_index_groups=near_groups, tiled=True
    ).reshape(-1, 8, 128)
    loss_sum = lax.dynamic_slice_in_dim(tiles[used, 0], dp_index * queries, queries, 0)
    pair_loss = loss_sum / count
    flat = tiles[:used].reshape(2 * rank // 8, wide // 128, 8, 128)
    flat = jnp.swapaxes(flat, 1, 2).reshape(2 * rank, wide)
    down_grad = flat[:rank].T
    up_weight_gradient = flat[rank:]
    return (context_grad, grad_rows, down_grad, up_weight_gradient, pair_loss)


def solution(mesh):
    in_specs = (
        P("dp", "cand", "tensor"),
        P("dp", ("cand", "tensor"), None),
        P("cand", "tensor"),
        P("tensor", None),
        P(),
        P(),
        P(),
        P("dp", "cand", "tensor"),
        P("dp", "cand", "tensor"),
        P("dp"),
    )
    out_specs = (
        P("dp", "cand", "tensor"),
        P("dp", ("cand", "tensor"), None),
        P("tensor", None),
        P(None, "tensor"),
        P("dp"),
    )
    return jax.shard_map(
        on_device, mesh=mesh, in_specs=in_specs, out_specs=out_specs, check_vma=False
    )
```
